32 devices in a mesh: lat: 8 (over z, x), lon: 4 (over y, core).
Axes of the slice: x: 2, y: 2, z: 4, core: 2. Of those that a mesh axis runs over, the one named last changes fastest.
Arguments:
- sky_map: bfloat16 [256, 8, 8192], P('lat', None, 'lon'), may hold values from -6 to 6
- legendre: bfloat16 [256, 2048, 512], P('lat', None, 'lon'), may hold values from -0.5 to 0.5
- conv_weight: bfloat16 [9, 8, 8], replicated, may hold values from -0.75 to 0.75
- block_ids: int32 [4], replicated, may hold values from 0 to 15, as said below
Outputs:
- harmonics: float32 [2048, 16, 512], P('lat', None, 'lon')
- local_conv: bfloat16 [256, 8, 8192], P('lat', None, 'lon')
The draws below stay inside these ranges and needn't reach their ends.
Inputs may be any that keep to these rules, and one draw needn't show every extreme that they name: `block_ids`: distinct m-block numbers in increasing order; the first is 0 and the last is 15.
All inputs are finite; a program needn't handle non-finite values.
Results may differ from the reference program's by a relative error of at most 0.0049.
Values may be sent and summed in bfloat16 or wider, within the bound.
A program may use at most 128 MiB of HBM per device.

```python
import jax
import jax.numpy as jnp
from jax import lax

C = 8
NPHI = 8192
L = 2048
MBLK = 128
KW = 4
R_DEV = 32
CYCLES = 256
NBLK = 4
M = 512
N_LAT = 8


def draw_block_ids(key, part):
    highest = L // MBLK - 1
    middle = jax.random.permutation(key, highest - 1)[:NBLK - 2] + 1
    middle = jnp.sort(middle).astype(jnp.int32)
    return jnp.concatenate([jnp.zeros((1,), jnp.int32), middle, jnp.full((1,), highest, jnp.int32)])


def strengthened(entries, key, source, target, shards_of, factor):
    owner, partner = [(jnp.arange(entries.shape[dim]) // (entries.shape[dim] // shards_of)).reshape([-1 if axis == dim else 1 for axis in range(entries.ndim)]) for dim in (source, target)]
    chosen = jax.random.permutation(key, shards_of)[partner]
    strong = (owner == chosen) | (owner == (partner + shards_of // 2) % shards_of)
    return jnp.where(strong, factor * entries, entries)


def shard_levels(stream_key, dims, pieces, low, largest):
    gain = 1.0
    for position, parts in pieces:
        steps = jax.random.uniform(jax.random.fold_in(jax.random.fold_in(stream_key, 6), position), (parts,), jnp.float32, low / len(pieces), largest / len(pieces))
        gain = gain * jnp.repeat(jnp.exp(steps), dims[position] // parts).reshape((-1,) + (1,) * (len(dims) - 1 - position))
    return gain


def normal_values(key, extent, width, reach, pieces=(), kind=jnp.bfloat16):
    array = width * jax.random.normal(key, extent, jnp.float32)
    if pieces:
        array = array * shard_levels(key, extent, pieces, -0.22, 0.18)
    return jnp.clip(array, -reach, reach).astype(kind)


def gaussian_with(stream_key, shape, deviation, limit, pieces, heavy, kind=jnp.bfloat16):
    array = deviation * jax.random.normal(stream_key, shape, jnp.float32)
    if pieces:
        array = array * shard_levels(stream_key, shape, pieces, -0.22, 0.18)
    return jnp.clip(strengthened(array, jax.random.fold_in(stream_key, 3), *heavy), -limit, limit).astype(kind)


def setup_inputs(seed: int = 0) -> dict:
    key_of = jax.random.split(jax.random.key(seed), 5)
    return {
        "sky_map": normal_values(key_of[0], (CYCLES, C, NPHI), 1.0, 6.0, ((0, 8), (2, 4))),
        "legendre": gaussian_with(key_of[1], (CYCLES, L, M), CYCLES ** -0.5, 0.5, ((0, 8), (2, 4)), (0, 1, 8, 2.0)),
        "conv_weight": normal_values(key_of[2], (2 * KW + 1, C, C), ((2 * KW + 1) * C) ** -0.5, 0.75),
        "block_ids": draw_block_ids(jax.random.fold_in(key_of[4], 71), 0),
    }


def fourier_table(orders, pixels, length):
    phases = (orders[:, None] * pixels[None, :]) % length
    angles = phases.astype(jnp.float32) * (2.0 * jnp.pi / length)
    factor = length ** -0.5
    cos_table = (jnp.cos(angles) * factor).astype(jnp.bfloat16)
    sin_table = (jnp.sin(angles) * factor).astype(jnp.bfloat16)
    return cos_table, sin_table


def reference(sky_map, legendre, conv_weight, block_ids):
    orders = (block_ids[:, None] * MBLK + jnp.arange(MBLK, dtype=jnp.int32)[None, :]).reshape(-1).astype(jnp.int32)
    pixels = jnp.arange(NPHI, dtype=jnp.int32)
    cos_table, sin_table = fourier_table(orders, pixels, NPHI)
    flat_rows = sky_map.reshape(CYCLES * C, NPHI)
    contract = (((1,), (1,)), ((), ()))
    real_part = lax.dot_general(cos_table, flat_rows, contract, preferred_element_type=jnp.float32)
    imag_part = -lax.dot_general(sin_table, flat_rows, contract, preferred_element_type=jnp.float32)
    fourier = jnp.stack([real_part, imag_part], axis=1).reshape(M, 2, CYCLES, C)
    spectra = jnp.transpose(fourier, (2, 1, 3, 0)).reshape(CYCLES, 2 * C, M).astype(jnp.bfloat16)
    band_tiles = legendre.reshape(N_LAT, R_DEV, L, M)
    band_spectra = spectra.reshape(N_LAT, R_DEV, 2 * C, M)

    def add_band(running, pair):
        tile_rows, spectra_rows = pair
        term = jnp.einsum("rlm,rkm->lkm", tile_rows.astype(jnp.float32), spectra_rows.astype(jnp.float32))
        return running + term, None

    total, _ = lax.scan(add_band, jnp.zeros((L, 2 * C, M), jnp.float32), (band_tiles, band_spectra))
    degree_ids = jnp.arange(L, dtype=jnp.int32)
    harmonics = jnp.where(degree_ids[:, None, None] >= orders[None, None, :], total, jnp.float32(0.0))
    padded = jnp.concatenate([sky_map[:, :, NPHI - KW:], sky_map, sky_map[:, :, :KW]], axis=2)
    pixel_sum = jnp.zeros((CYCLES, C, NPHI), jnp.float32)
    for offset in range(2 * KW + 1):
        pixel_sum = pixel_sum + jnp.einsum("oc,rcp->rop", conv_weight[offset].astype(jnp.float32), padded[:, :, offset:offset + NPHI].astype(jnp.float32))
    local_conv = pixel_sum.astype(jnp.bfloat16)
    return harmonics, local_conv
```

```python
import functools
import itertools

import jax
import jax.numpy as jnp
from jax import lax
from jax.experimental import pallas as pl
from jax.experimental.pallas import tpu as pltpu
from jax.sharding import PartitionSpec as P

TILE = 16
PIECE = 32
LEAD = 8
LAG = 4
WINDOW = 6
FLOORS = ((1, 2),)


def rotated(shard, axis, by):
    peers = lax.axis_size(axis)
    return lax.ppermute(shard, axis, [(i, (i + by) % peers) for i in range(peers)])


def padded_cycle(block, width):
    low = rotated(block[:, :, -width:], "lon", 1)
    high = rotated(block[:, :, :width], "lon", -1)
    fill = jnp.zeros(block.shape[:2] + (128 - 2 * width,), block.dtype)
    return jnp.concatenate([low, block, high, fill], axis=2)


def angle_pair(phases, length):
    angles = phases.astype(jnp.float32) * (2.0 * jnp.pi / length)
    return jnp.cos(angles), jnp.sin(angles)


def fourier_tables(orders, first_pixel, segment, length):
    fine = 128
    coarse_pixels = first_pixel + fine * jnp.arange(segment // fine, dtype=jnp.int32)
    fine_pixels = jnp.arange(fine, dtype=jnp.int32)
    cos_a, sin_a = angle_pair((orders[:, None] * coarse_pixels[None, :]) % length, length)
    cos_b, sin_b = angle_pair((orders[:, None] * fine_pixels[None, :]) % length, length)
    factor = length ** (-0.5)
    cos_a, sin_a = (cos_a * factor)[:, :, None], (sin_a * factor)[:, :, None]
    cos_b, sin_b = cos_b[:, None, :], sin_b[:, None, :]
    cos_table = (cos_a * cos_b - sin_a * sin_b).astype(jnp.bfloat16)
    sin_table = (sin_a * cos_b + cos_a * sin_b).astype(jnp.bfloat16)
    shape = (orders.shape[0], segment)
    return cos_table.reshape(shape), sin_table.reshape(shape)


def chunk_at(e, z, n):
    low, high = jnp.minimum(z, n - 1 - z), jnp.maximum(z, n - 1 - z)
    single = e < high - low
    late = e - (high - low)
    step = jnp.where(single, low + e, high + late // 2)
    upward = jnp.where(single, 2 * z < n - 1, late % 2 == 0)
    return jnp.where(upward, n - 1 - step + z, step - (n - 1) + z)


class Plan:
    def __init__(self, floors, lon_count, n, degrees, width):
        self.n, self.half = n, lon_count // 2
        self.share = degrees // (2 * n)
        self.piece = min(self.share, PIECE)
        self.split = self.share // self.piece
        self.slabs = n * self.split
        self.first = [floor * width for floor in floors]
        self.handed = min(
            itertools.product(range(self.split // 2 + 1), repeat=self.half), key=self.load
        )
        self.ranks = max(1, *self.handed)
        self.guests = n * self.ranks
        self.jobs = self.slabs + self.guests

    def load(self, handed):
        n, half, split = self.n, self.half, self.split
        across, pairs = [0, 0, 0], {}
        chain = {}
        for lon, first in enumerate(self.first):
            for chunk, side, q in itertools.product(range(n), range(2), range(split)):
                if ((chunk * 2 + side) * split + q + 1) * self.piece <= first:
                    continue
                over = lon < half and (q * handed[lon % half]) % split < handed[lon % half]
                y = 1 if lon >= half or over else 0
                across[0] += over
                pairs[y, side] = pairs.get((y, side), 0) + 1
                for z in range(n):
                    if z != chunk:
                        key = y, side, z, z < chunk
                        chain[key] = chain.get(key, 0) + 1
        return max([across[0], *pairs.values(), *chain.values()]), across[0]


def lat_kernel(
    plan, leg_ref, spec_ref, weight_ref, padded_ref, out_ref, conv_ref,
    leg_buf, send, got, guest_in, total, chain_out, chain_in, back_out, back_in,
    leg_sem, send_sem, got_sem, guest_sem, pass_sem, chain_send, chain_recv, back_send, back_recv,
):
    n, half, piece, split = plan.n, plan.half, plan.piece, plan.split
    slabs, ranks, jobs = plan.slabs, plan.ranks, plan.jobs
    lat = lax.axis_index("lat")
    z, x = lat // 2, lat % 2
    rows, parts = spec_ref.shape[0], spec_ref.shape[1]
    lon = lax.axis_index("lon")
    lower = lon < half
    across = jnp.where(lower, lon + half, lon - half)

    def chosen(table, index):
        value = table[0]
        for k in range(1, len(table)):
            value = jnp.where(index == k, table[k], value)
        return value

    own_first, guest_first = chosen(plan.first, lon), chosen(plan.first, across)
    count = chosen(plan.handed, lon % half)

    barrier = pltpu.get_barrier_semaphore()

    def greet(**device):
        pl.semaphore_signal(barrier, inc=1, device_id=device)

    greet(lat=z * 2 + 1 - x)
    greet(lon=across)

    @pl.when(z > 0)
    def _():
        greet(lat=lat - 2)

    @pl.when(z < n - 1)
    def _():
        greet(lat=lat + 2)

    def place(i):
        return chunk_at(i // split, z, n), i % split

    def needed(first, chunk, side, q):
        return ((chunk * 2 + side) * split + q + 1) * piece > first

    def handed(q):
        return (q * count) % split < count

    def seat(chunk, q):
        return chunk * ranks + (q * count) // split

    def load(i):
        chunk, q = place(i)
        return pltpu.make_async_copy(
            leg_ref.at[:, pl.ds(chunk * 2, 2), pl.ds(pl.multiple_of(q * piece, piece), piece), :],
            leg_buf.at[i],
            leg_sem.at[i],
        )

    def loaded(i):
        chunk, q = place(i)
        return needed(own_first, chunk, 1, q)

    def start_load(i):
        @pl.when(loaded(i))
        def _():
            load(i).start()

    def remote(source, target, send_at, recv_at, **device):
        return pltpu.make_async_remote_copy(
            src_ref=source, dst_ref=target, send_sem=send_at, recv_sem=recv_at, device_id=device
        )

    partner = z * 2 + 1 - x

    def pair_copy(job):
        return remote(send.at[job], got.at[job], send_sem.at[job], got_sem.at[job], lat=partner)

    def hand_copy(j, chunk, q):
        spot = seat(chunk, q)
        slot = jnp.where(j == 0, chunk * split + q, slabs + spot)
        return remote(
            send.at[slot], guest_in.at[j, spot], send_sem.at[slot], guest_sem.at[j, spot], lon=across
        )

    def pass_copy(spot):
        return remote(
            guest_in.at[0, spot], got.at[slabs + spot], pass_sem.at[spot],
            got_sem.at[slabs + spot], lat=partner,
        )

    def chain_copy(job, chunk, extra):
        onward = jnp.where(z < chunk, 1, -1)
        slot = jnp.where((z > chunk) & (z - 1 == chunk), extra, job)
        target = jnp.clip(lat + 2 * onward, 0, 2 * n - 1)
        return remote(
            chain_out.at[job], chain_in.at[slot], chain_send.at[job], chain_recv.at[slot], lat=target
        )

    def chain_arrived(slot):
        return remote(
            chain_out.at[0], chain_in.at[slot], chain_send.at[0], chain_recv.at[slot], lat=partner
        )

    def back_copy(rank):
        return remote(
            back_out.at[rank], back_in.at[rank], back_send.at[rank], back_recv.at[rank], lon=across
        )

    def contract(i, side, write):
        @pl.loop(0, piece // TILE)
        def _(tile):
            span = pl.ds(pl.multiple_of(tile * TILE, TILE), TILE)
            sums = [None] * parts
            for r in range(rows):
                leg = leg_buf[i, r, side, span, :].astype(jnp.float32)
                leg = leg.reshape(TILE // 8, 8, -1)
                for k in range(parts):
                    term = leg * spec_ref[r, k][None]
                    sums[k] = term if sums[k] is None else sums[k] + term
            for k in range(parts):
                write(k, span, sums[k].reshape(TILE, -1))

    cycles, _, segment = conv_ref.shape
    batch = -(-cycles // slabs)
    taps = weight_ref.shape[1] // padded_ref.shape[1]

    def convolve(r):
        row = padded_ref[r].astype(jnp.float32)
        wide = row.shape[1]
        shifted = [row] + [pltpu.roll(row, wide - t, 1) for t in range(1, taps)]
        windows = jnp.concatenate([w[:, :segment] for w in shifted], axis=0)
        conv_ref[r] = jnp.dot(
            weight_ref[...], windows.astype(jnp.bfloat16), preferred_element_type=jnp.float32
        ).astype(conv_ref.dtype)

    def produce(i):
        chunk, q = place(i)
        job = chunk * split + q
        over = lower & handed(q)

        @pl.when(i + WINDOW < slabs)
        def _():
            start_load(i + WINDOW)

        @pl.when(loaded(i))
        def _():
            load(i).wait()

        @pl.loop(0, 1 + jnp.where(over, 1, 0))
        def _(j):
            side = jnp.where(j == 0, 1 - x, x)

            @pl.when(needed(own_first, chunk, side, q))
            def _():
                slot = jnp.where(j == 0, job, slabs + seat(chunk, q))

                def write(k, span, value):
                    send[slot, k, span, :] = value.astype(send.dtype)

                contract(i, side, write)

                @pl.when(over)
                def _():
                    hand_copy(j, chunk, q).start()

                @pl.when(jnp.logical_not(over))
                def _():
                    pair_copy(job).start()

    def passes(chunk, q):
        return jnp.logical_not(lower) & handed(q) & needed(guest_first, chunk, 1 - x, q)

    def hosts(chunk, q):
        return jnp.logical_not(lower) & handed(q) & needed(guest_first, chunk, x, q)

    def keeps(chunk, q):
        return jnp.logical_not(lower & handed(q)) & needed(own_first, chunk, x, q)

    def pass_on(i):
        chunk, q = place(i)

        @pl.when(passes(chunk, q))
        def _():
            spot = seat(chunk, q)
            hand_copy(0, chunk, q).wait_recv()
            pass_copy(spot).start()

    def accumulate(buffer, slot):
        @pl.loop(0, parts)
        def _(k):
            total[k] = total[k] + buffer[slot, k].astype(jnp.float32)

    def settle(job, extra, chunk, finish):
        pair_copy(job).wait_recv()
        accumulate(got, job)

        @pl.when(((z <= chunk) & (z > 0)) | ((z > chunk) & (z < n - 1)))
        def _():
            chain_arrived(job).wait_recv()
            accumulate(chain_in, job)

        @pl.when((z == chunk) & (z < n - 1))
        def _():
            chain_arrived(extra).wait_recv()
            accumulate(chain_in, extra)

        @pl.when(z != chunk)
        def _():
            @pl.loop(0, parts)
            def _(k):
                chain_out[job, k] = total[k].astype(chain_out.dtype)

            chain_copy(job, chunk, extra).start()

        pl.when(z == chunk)(finish)

    def rows_of(q):
        return pl.ds(pl.multiple_of(q * piece, piece), piece)

    def consume(i):
        chunk, q = place(i)
        job = chunk * split + q

        @pl.when(keeps(chunk, q))
        def _():
            def write(k, span, value):
                total[k, span, :] = value

            contract(i, x, write)

            def finish():
                for k in range(parts):
                    out_ref[rows_of(q), k, :] = total[k]

            settle(job, jobs + q, chunk, finish)

        @pl.when((z == chunk) & jnp.logical_not(needed(own_first, chunk, x, q)))
        def _():
            for k in range(parts):
                out_ref[rows_of(q), k, :] = jnp.zeros((piece, out_ref.shape[2]), out_ref.dtype)

        @pl.when(hosts(chunk, q))
        def _():
            spot = seat(chunk, q)
            hand_copy(1, chunk, q).wait_recv()

            @pl.loop(0, parts)
            def _(k):
                total[k] = guest_in[1, spot, k].astype(jnp.float32)

            rank = spot - chunk * ranks

            def finish():
                @pl.loop(0, parts)
                def _(k):
                    back_out[rank, k] = total[k].astype(back_out.dtype)

                back_copy(rank).start()

            settle(slabs + spot, jobs + split + rank, chunk, finish)

    @pl.loop(0, min(WINDOW, slabs))
    def _(i):
        start_load(i)

    pl.semaphore_wait(barrier, 2 + jnp.minimum(z, 1) + jnp.minimum(n - 1 - z, 1))

    @pl.loop(0, slabs + LEAD)
    def _(t):
        @pl.when(t < slabs)
        def _():
            produce(t)

        @pl.when((t >= LAG) & (t < slabs + LAG))
        def _():
            pass_on(t - LAG)

        @pl.when(t >= LEAD)
        def _():
            consume(t - LEAD)

        @pl.loop(0, batch)
        def _(j):
            @pl.when(t * batch + j < cycles)
            def _():
                convolve(jnp.minimum(t * batch + j, cycles - 1))

    @pl.loop(0, split)
    def _(q):
        @pl.when(lower & handed(q) & needed(own_first, z, x, q))
        def _():
            rank = seat(z, q) - z * ranks
            back_copy(rank).wait_recv()
            for k in range(parts):
                out_ref[rows_of(q), k, :] = back_in[rank, k].astype(out_ref.dtype)

    @pl.loop(0, slabs)
    def _(i):
        chunk, q = place(i)
        job, spot = chunk * split + q, seat(chunk, q)
        over = lower & handed(q)

        @pl.when(needed(own_first, chunk, 1 - x, q))
        def _():
            @pl.when(over)
            def _():
                hand_copy(0, chunk, q).wait_send()

            @pl.when(jnp.logical_not(over))
            def _():
                pair_copy(job).wait_send()

        @pl.when(over & needed(own_first, chunk, x, q))
        def _():
            hand_copy(1, chunk, q).wait_send()

        @pl.when(passes(chunk, q))
        def _():
            pass_copy(spot).wait_send()

        @pl.when(keeps(chunk, q) & (z != chunk))
        def _():
            chain_copy(job, chunk, jobs + q).wait_send()

        @pl.when(hosts(chunk, q))
        def _():
            rank = spot - chunk * ranks

            @pl.when(z != chunk)
            def _():
                chain_copy(slabs + spot, chunk, jobs + split + rank).wait_send()

            @pl.when(z == chunk)
            def _():
                back_copy(rank).wait_send()


def lat_sums(plan, number, legendre, spec_rows, weights, padded, conv_shape):
    rows, degrees, width = legendre.shape
    parts = spec_rows.shape[1]
    legendre = legendre.reshape(rows, 2 * plan.n, plan.share, width)
    block = (parts, plan.piece, width)
    wire = jnp.bfloat16
    dma = pltpu.SemaphoreType.DMA
    arrivals = plan.jobs + plan.split + plan.ranks
    return pl.pallas_call(
        functools.partial(lat_kernel, plan),
        out_shape=(
            jax.ShapeDtypeStruct((plan.share, parts, width), jnp.float32),
            jax.ShapeDtypeStruct(conv_shape, jnp.bfloat16),
        ),
        in_specs=[pl.BlockSpec(memory_space=pl.ANY)]
        + [pl.BlockSpec(memory_space=pltpu.VMEM)] * 3,
        out_specs=[pl.BlockSpec(memory_space=pltpu.VMEM)] * 2,
        scratch_shapes=[
            pltpu.VMEM((plan.slabs, rows, 2, plan.piece, width), legendre.dtype),
            pltpu.VMEM((plan.jobs, *block), wire),
            pltpu.VMEM((plan.jobs, *block), wire),
            pltpu.VMEM((2, plan.guests, *block), wire),
            pltpu.VMEM(block, jnp.float32),
            pltpu.VMEM((plan.jobs, *block), wire),
            pltpu.VMEM((arrivals, *block), wire),
            pltpu.VMEM((plan.ranks, *block), wire),
            pltpu.VMEM((plan.ranks, *block), wire),
            dma((plan.slabs,)),
            dma((plan.jobs,)),
            dma((plan.jobs,)),
            dma((2, plan.guests)),
            dma((plan.guests,)),
            dma((plan.jobs,)),
            dma((arrivals,)),
            dma((plan.ranks,)),
            dma((plan.ranks,)),
        ],
        compiler_params=pltpu.CompilerParams(
            collective_id=number, has_side_effects=True, vmem_limit_bytes=63 * 2**20
        ),
        cost_estimate=pl.CostEstimate(
            flops=10**10, bytes_accessed=legendre.size * 2, transcendentals=0
        ),
    )(legendre, spec_rows, weights, padded)


def on_device(sky_map, legendre, conv_weight, block_ids):
    cycles_dev, channels, segment = sky_map.shape
    lat_count, lon_count = lax.axis_size("lat"), lax.axis_size("lon")
    lat_index, lon_index = lax.axis_index("lat"), lax.axis_index("lon")
    degrees, block_size = legendre.shape[1:]
    length = segment * lon_count
    orders = (
        block_ids[:, None] * block_size + jnp.arange(block_size, dtype=jnp.int32)[None, :]
    ).reshape(-1)
    width = conv_weight.shape[0] // 2

    flat_rows = sky_map.reshape(cycles_dev * channels, segment)
    cos_table, sin_table = fourier_tables(orders, lon_index * segment, segment, length)
    contract = (((1,), (1,)), ((), ()))
    real_part = lax.dot_general(flat_rows, cos_table, contract, preferred_element_type=jnp.float32)
    imag_part = -lax.dot_general(flat_rows, sin_table, contract, preferred_element_type=jnp.float32)

    def m_block(owner):
        return jnp.stack(
            [
                lax.dynamic_slice_in_dim(part, owner * block_size, block_size, 1)
                for part in (real_part, imag_part)
            ]
        )

    sums = m_block(lon_index)
    arrived = [
        rotated(m_block((lon_index + by) % lon_count).astype(jnp.bfloat16), "lon", by)
        for by in range(1, lon_count)
    ]
    for block in arrived:
        sums = sums + block.astype(jnp.float32)
    spectra = sums.astype(jnp.bfloat16).reshape(2, cycles_dev, channels, block_size)
    spectra = jnp.transpose(spectra, (1, 0, 2, 3)).reshape(cycles_dev, 2 * channels, 1, block_size)
    spec_rows = jnp.broadcast_to(
        spectra.astype(jnp.float32), (cycles_dev, 2 * channels, 8, block_size)
    )

    share = degrees // lat_count
    padded = padded_cycle(sky_map, width)
    weights = jnp.transpose(conv_weight, (1, 0, 2)).reshape(channels, -1)
    operands = legendre, spec_rows, weights, padded
    highest = degrees // block_size - 1
    choices = [(0, *middle, highest) for middle in FLOORS]
    if len(choices[0]) != lon_count:
        choices = [tuple(range(lon_count))]
    builds = [
        functools.partial(
            lat_sums,
            Plan(floors, lon_count, lat_count // 2, degrees, block_size),
            number,
            conv_shape=sky_map.shape,
        )
        for number, floors in enumerate(choices)
    ]
    if len(builds) == 1:
        summed, local_conv = builds[0](*operands)
    else:
        fits = jnp.all(jnp.array(choices, jnp.int32) <= block_ids[None, :], axis=1)
        best = jnp.max(jnp.where(fits, jnp.arange(len(choices), dtype=jnp.int32), 0))
        summed, local_conv = lax.switch(best, builds, *operands)
    degree_ids = lat_index * share + jnp.arange(share, dtype=jnp.int32)
    own_orders = lax.dynamic_slice_in_dim(orders, lon_index * block_size, block_size, 0)
    harmonics = jnp.where(
        degree_ids[:, None, None] >= own_orders[None, None, :], summed, jnp.float32(0.0)
    )
    return harmonics, local_conv


def solution(mesh):
    return jax.shard_map(
        on_device,
        mesh=mesh,
        in_specs=(P("lat", None, "lon"), P("lat", None, "lon"), P(), P()),
        out_specs=(P("lat", None, "lon"), P("lat", None, "lon")),
        check_vma=False,
    )
```

```python
import functools
import itertools

import jax
import jax.numpy as jnp
from jax import lax
from jax.experimental import pallas as pl
from jax.experimental.pallas import tpu as pltpu
from jax.sharding import PartitionSpec as P

TILE = 16
PIECE = 32
LEAD = 8
LAG = 4
WINDOW = 6
FLOORS = ((1, 2), (1, 7), (4, 8), (8, 11))


def rotated(shard, axis, by):
    peers = lax.axis_size(axis)
    return lax.ppermute(shard, axis, [(i, (i + by) % peers) for i in range(peers)])


def padded_cycle(block, width):
    low = rotated(block[:, :, -width:], "lon", 1)
    high = rotated(block[:, :, :width], "lon", -1)
    fill = jnp.zeros(block.shape[:2] + (128 - 2 * width,), block.dtype)
    return jnp.concatenate([low, block, high, fill], axis=2)


def angle_pair(phases, length):
    angles = phases.astype(jnp.float32) * (2.0 * jnp.pi / length)
    return jnp.cos(angles), jnp.sin(angles)


def fourier_tables(orders, first_pixel, segment, length):
    fine = 128
    coarse_pixels = first_pixel + fine * jnp.arange(segment // fine, dtype=jnp.int32)
    fine_pixels = jnp.arange(fine, dtype=jnp.int32)
    cos_a, sin_a = angle_pair((orders[:, None] * coarse_pixels[None, :]) % length, length)
    cos_b, sin_b = angle_pair((orders[:, None] * fine_pixels[None, :]) % length, length)
    factor = length ** (-0.5)
    cos_a, sin_a = (cos_a * factor)[:, :, None], (sin_a * factor)[:, :, None]
    cos_b, sin_b = cos_b[:, None, :], sin_b[:, None, :]
    cos_table = (cos_a * cos_b - sin_a * sin_b).astype(jnp.bfloat16)
    sin_table = (sin_a * cos_b + cos_a * sin_b).astype(jnp.bfloat16)
    shape = (orders.shape[0], segment)
    return cos_table.reshape(shape), sin_table.reshape(shape)


def chunk_at(e, z, n):
    low, high = jnp.minimum(z, n - 1 - z), jnp.maximum(z, n - 1 - z)
    single = e < high - low
    late = e - (high - low)
    step = jnp.where(single, low + e, high + late // 2)
    upward = jnp.where(single, 2 * z < n - 1, late % 2 == 0)
    return jnp.where(upward, n - 1 - step + z, step - (n - 1) + z)


class Plan:
    def __init__(self, floors, lon_count, n, degrees, width):
        self.n, self.half = n, lon_count // 2
        self.share = degrees // (2 * n)
        self.piece = min(self.share, PIECE)
        self.split = self.share // self.piece
        self.slabs = n * self.split
        self.first = [floor * width for floor in floors]
        counts = list(itertools.product(range(self.split // 2 + 1), repeat=self.half))
        self.handed = [
            min(counts, key=functools.partial(self.load, chunk)) for chunk in range(n)
        ]
        self.ranks = max(1, *itertools.chain(*self.handed))
        self.guests = n * self.ranks
        self.jobs = self.slabs + self.guests

    def load(self, chunk, handed):
        half, split = self.half, self.split
        across, pairs, cores = 0, [0] * 4, [0] * (2 * half)
        for lon, first in enumerate(self.first):
            for side, q in itertools.product(range(2), range(split)):
                if ((chunk * 2 + side) * split + q + 1) * self.piece <= first:
                    continue
                over = lon < half and (q * handed[lon % half]) % split < handed[lon % half]
                across += over
                pairs[2 * (lon >= half or over) + side] += 1
                cores[lon + half * over] += 1
        return max(across, *pairs), max(cores), across


def lat_kernel(
    plan, leg_ref, spec_ref, weight_ref, padded_ref, out_ref, conv_ref,
    leg_buf, send, got, guest_in, total, chain_out, chain_in, back_out, back_in,
    leg_sem, send_sem, got_sem, guest_sem, pass_sem, chain_send, chain_recv, back_send, back_recv,
):
    n, half, piece, split = plan.n, plan.half, plan.piece, plan.split
    slabs, ranks, jobs = plan.slabs, plan.ranks, plan.jobs
    lat = lax.axis_index("lat")
    z, x = lat // 2, lat % 2
    rows, parts = spec_ref.shape[0], spec_ref.shape[1]
    lon = lax.axis_index("lon")
    lower = lon < half
    across = jnp.where(lower, lon + half, lon - half)

    def chosen(table, index):
        value = table[0]
        for k in range(1, len(table)):
            value = jnp.where(index == k, table[k], value)
        return value

    own_first, guest_first = chosen(plan.first, lon), chosen(plan.first, across)
    counts = [chosen(handed, lon % half) for handed in plan.handed]

    barrier = pltpu.get_barrier_semaphore()

    def greet(**device):
        pl.semaphore_signal(barrier, inc=1, device_id=device)

    greet(lat=z * 2 + 1 - x)
    greet(lon=across)

    @pl.when(z > 0)
    def _():
        greet(lat=lat - 2)

    @pl.when(z < n - 1)
    def _():
        greet(lat=lat + 2)

    def place(i):
        return chunk_at(i // split, z, n), i % split

    def needed(first, chunk, side, q):
        return ((chunk * 2 + side) * split + q + 1) * piece > first

    def handed(chunk, q):
        count = chosen(counts, chunk)
        return (q * count) % split < count

    def seat(chunk, q):
        return chunk * ranks + (q * chosen(counts, chunk)) // split

    def load(i):
        chunk, q = place(i)
        return pltpu.make_async_copy(
            leg_ref.at[:, pl.ds(chunk * 2, 2), pl.ds(pl.multiple_of(q * piece, piece), piece), :],
            leg_buf.at[i],
            leg_sem.at[i],
        )

    def loaded(i):
        chunk, q = place(i)
        return needed(own_first, chunk, 1, q)

    def start_load(i):
        @pl.when(loaded(i))
        def _():
            load(i).start()

    def remote(source, target, send_at, recv_at, **device):
        return pltpu.make_async_remote_copy(
            src_ref=source, dst_ref=target, send_sem=send_at, recv_sem=recv_at, device_id=device
        )

    partner = z * 2 + 1 - x

    def pair_copy(job):
        return remote(send.at[job], got.at[job], send_sem.at[job], got_sem.at[job], lat=partner)

    def hand_copy(j, chunk, q):
        spot = seat(chunk, q)
        slot = jnp.where(j == 0, chunk * split + q, slabs + spot)
        return remote(
            send.at[slot], guest_in.at[j, spot], send_sem.at[slot], guest_sem.at[j, spot], lon=across
        )

    def pass_copy(spot):
        return remote(
            guest_in.at[0, spot], got.at[slabs + spot], pass_sem.at[spot],
            got_sem.at[slabs + spot], lat=partner,
        )

    def chain_copy(job, chunk, extra):
        onward = jnp.where(z < chunk, 1, -1)
        slot = jnp.where((z > chunk) & (z - 1 == chunk), extra, job)
        target = jnp.clip(lat + 2 * onward, 0, 2 * n - 1)
        return remote(
            chain_out.at[job], chain_in.at[slot], chain_send.at[job], chain_recv.at[slot], lat=target
        )

    def chain_arrived(slot):
        return remote(
            chain_out.at[0], chain_in.at[slot], chain_send.at[0], chain_recv.at[slot], lat=partner
        )

    def back_copy(rank):
        return remote(
            back_out.at[rank], back_in.at[rank], back_send.at[rank], back_recv.at[rank], lon=across
        )

    def contract(i, side, write):
        @pl.loop(0, piece // TILE)
        def _(tile):
            span = pl.ds(pl.multiple_of(tile * TILE, TILE), TILE)
            sums = [None] * parts
            for r in range(rows):
                leg = leg_buf[i, r, side, span, :].astype(jnp.float32)
                leg = leg.reshape(TILE // 8, 8, -1)
                for k in range(parts):
                    term = leg * spec_ref[r, k][None]
                    sums[k] = term if sums[k] is None else sums[k] + term
            for k in range(parts):
                write(k, span, sums[k].reshape(TILE, -1))

    cycles, _, segment = conv_ref.shape
    batch = -(-cycles // slabs)
    taps = weight_ref.shape[1] // padded_ref.shape[1]

    def convolve(r):
        row = padded_ref[r].astype(jnp.float32)
        wide = row.shape[1]
        shifted = [row] + [pltpu.roll(row, wide - t, 1) for t in range(1, taps)]
        windows = jnp.concatenate([w[:, :segment] for w in shifted], axis=0)
        conv_ref[r] = jnp.dot(
            weight_ref[...], windows.astype(jnp.bfloat16), preferred_element_type=jnp.float32
        ).astype(conv_ref.dtype)

    def produce(i):
        chunk, q = place(i)
        job = chunk * split + q
        over = lower & handed(chunk, q)

        @pl.when(i + WINDOW < slabs)
        def _():
            start_load(i + WINDOW)

        @pl.when(loaded(i))
        def _():
            load(i).wait()

        @pl.loop(0, 1 + jnp.where(over, 1, 0))
        def _(j):
            side = jnp.where(j == 0, 1 - x, x)

            @pl.when(needed(own_first, chunk, side, q))
            def _():
                slot = jnp.where(j == 0, job, slabs + seat(chunk, q))

                def write(k, span, value):
                    send[slot, k, span, :] = value.astype(send.dtype)

                contract(i, side, write)

                @pl.when(over)
                def _():
                    hand_copy(j, chunk, q).start()

                @pl.when(jnp.logical_not(over))
                def _():
                    pair_copy(job).start()

    def passes(chunk, q):
        return jnp.logical_not(lower) & handed(chunk, q) & needed(guest_first, chunk, 1 - x, q)

    def hosts(chunk, q):
        return jnp.logical_not(lower) & handed(chunk, q) & needed(guest_first, chunk, x, q)

    def keeps(chunk, q):
        return jnp.logical_not(lower & handed(chunk, q)) & needed(own_first, chunk, x, q)

    def pass_on(i):
        chunk, q = place(i)

        @pl.when(passes(chunk, q))
        def _():
            spot = seat(chunk, q)
            hand_copy(0, chunk, q).wait_recv()
            pass_copy(spot).start()

    def accumulate(buffer, slot):
        for k in range(parts):
            total[k] = total[k] + buffer[slot, k].astype(jnp.float32)

    def settle(job, extra, chunk, finish):
        pair_copy(job).wait_recv()
        accumulate(got, job)

        @pl.when(((z <= chunk) & (z > 0)) | ((z > chunk) & (z < n - 1)))
        def _():
            chain_arrived(job).wait_recv()
            accumulate(chain_in, job)

        @pl.when((z == chunk) & (z < n - 1))
        def _():
            chain_arrived(extra).wait_recv()
            accumulate(chain_in, extra)

        @pl.when(z != chunk)
        def _():
            for k in range(parts):
                chain_out[job, k] = total[k].astype(chain_out.dtype)

            chain_copy(job, chunk, extra).start()

        pl.when(z == chunk)(finish)

    def rows_of(q):
        return pl.ds(pl.multiple_of(q * piece, piece), piece)

    def consume(i):
        chunk, q = place(i)
        job = chunk * split + q

        @pl.when(keeps(chunk, q))
        def _():
            def write(k, span, value):
                total[k, span, :] = value

            contract(i, x, write)

            def finish():
                for k in range(parts):
                    out_ref[rows_of(q), k, :] = total[k]

            settle(job, jobs + q, chunk, finish)

        @pl.when((z == chunk) & jnp.logical_not(needed(own_first, chunk, x, q)))
        def _():
            for k in range(parts):
                out_ref[rows_of(q), k, :] = jnp.zeros((piece, out_ref.shape[2]), out_ref.dtype)

        @pl.when(hosts(chunk, q))
        def _():
            spot = seat(chunk, q)
            hand_copy(1, chunk, q).wait_recv()

            for k in range(parts):
                total[k] = guest_in[1, spot, k].astype(jnp.float32)

            rank = spot - chunk * ranks

            def finish():
                for k in range(parts):
                    back_out[rank, k] = total[k].astype(back_out.dtype)

                back_copy(rank).start()

            settle(slabs + spot, jobs + split + rank, chunk, finish)

    @pl.loop(0, min(WINDOW, slabs))
    def _(i):
        start_load(i)

    pl.semaphore_wait(barrier, 2 + jnp.minimum(z, 1) + jnp.minimum(n - 1 - z, 1))

    @pl.loop(0, slabs + LEAD)
    def _(t):
        @pl.when(t < slabs)
        def _():
            produce(t)

        @pl.when((t >= LAG) & (t < slabs + LAG))
        def _():
            pass_on(t - LAG)

        @pl.when(t >= LEAD)
        def _():
            consume(t - LEAD)

        @pl.loop(0, batch)
        def _(j):
            @pl.when(t * batch + j < cycles)
            def _():
                convolve(jnp.minimum(t * batch + j, cycles - 1))

    @pl.loop(0, split)
    def _(q):
        @pl.when(lower & handed(z, q) & needed(own_first, z, x, q))
        def _():
            rank = seat(z, q) - z * ranks
            back_copy(rank).wait_recv()
            for k in range(parts):
                out_ref[rows_of(q), k, :] = back_in[rank, k].astype(out_ref.dtype)

    @pl.loop(0, slabs)
    def _(i):
        chunk, q = place(i)
        job, spot = chunk * split + q, seat(chunk, q)
        over = lower & handed(chunk, q)

        @pl.when(needed(own_first, chunk, 1 - x, q))
        def _():
            @pl.when(over)
            def _():
                hand_copy(0, chunk, q).wait_send()

            @pl.when(jnp.logical_not(over))
            def _():
                pair_copy(job).wait_send()

        @pl.when(over & needed(own_first, chunk, x, q))
        def _():
            hand_copy(1, chunk, q).wait_send()

        @pl.when(passes(chunk, q))
        def _():
            pass_copy(spot).wait_send()

        @pl.when(keeps(chunk, q) & (z != chunk))
        def _():
            chain_copy(job, chunk, jobs + q).wait_send()

        @pl.when(hosts(chunk, q))
        def _():
            rank = spot - chunk * ranks

            @pl.when(z != chunk)
            def _():
                chain_copy(slabs + spot, chunk, jobs + split + rank).wait_send()

            @pl.when(z == chunk)
            def _():
                back_copy(rank).wait_send()


def lat_sums(plan, number, legendre, spec_rows, weights, padded, conv_shape):
    rows, degrees, width = legendre.shape
    parts = spec_rows.shape[1]
    legendre = legendre.reshape(rows, 2 * plan.n, plan.share, width)
    block = (parts, plan.piece, width)
    wire = jnp.bfloat16
    dma = pltpu.SemaphoreType.DMA
    arrivals = plan.jobs + plan.split + plan.ranks
    return pl.pallas_call(
        functools.partial(lat_kernel, plan),
        out_shape=(
            jax.ShapeDtypeStruct((plan.share, parts, width), jnp.float32),
            jax.ShapeDtypeStruct(conv_shape, jnp.bfloat16),
        ),
        in_specs=[pl.BlockSpec(memory_space=pl.ANY)]
        + [pl.BlockSpec(memory_space=pltpu.VMEM)] * 3,
        out_specs=[pl.BlockSpec(memory_space=pltpu.VMEM)] * 2,
        scratch_shapes=[
            pltpu.VMEM((plan.slabs, rows, 2, plan.piece, width), legendre.dtype),
            pltpu.VMEM((plan.jobs, *block), wire),
            pltpu.VMEM((plan.jobs, *block), wire),
            pltpu.VMEM((2, plan.guests, *block), wire),
            pltpu.VMEM(block, jnp.float32),
            pltpu.VMEM((plan.jobs, *block), wire),
            pltpu.VMEM((arrivals, *block), wire),
            pltpu.VMEM((plan.ranks, *block), wire),
            pltpu.VMEM((plan.ranks, *block), wire),
            dma((plan.slabs,)),
            dma((plan.jobs,)),
            dma((plan.jobs,)),
            dma((2, plan.guests)),
            dma((plan.guests,)),
            dma((plan.jobs,)),
            dma((arrivals,)),
            dma((plan.ranks,)),
            dma((plan.ranks,)),
        ],
        compiler_params=pltpu.CompilerParams(
            collective_id=number, has_side_effects=True, vmem_limit_bytes=63 * 2**20
        ),
        cost_estimate=pl.CostEstimate(
            flops=10**10, bytes_accessed=legendre.size * 2, transcendentals=0
        ),
    )(legendre, spec_rows, weights, padded)


def on_device(sky_map, legendre, conv_weight, block_ids):
    cycles_dev, channels, segment = sky_map.shape
    lat_count, lon_count = lax.axis_size("lat"), lax.axis_size("lon")
    lat_index, lon_index = lax.axis_index("lat"), lax.axis_index("lon")
    degrees, block_size = legendre.shape[1:]
    length = segment * lon_count
    orders = (
        block_ids[:, None] * block_size + jnp.arange(block_size, dtype=jnp.int32)[None, :]
    ).reshape(-1)
    width = conv_weight.shape[0] // 2

    flat_rows = sky_map.reshape(cycles_dev * channels, segment)
    cos_table, sin_table = fourier_tables(orders, lon_index * segment, segment, length)
    contract = (((1,), (1,)), ((), ()))
    real_part = lax.dot_general(flat_rows, cos_table, contract, preferred_element_type=jnp.float32)
    imag_part = -lax.dot_general(flat_rows, sin_table, contract, preferred_element_type=jnp.float32)

    def m_block(owner):
        return jnp.stack(
            [
                lax.dynamic_slice_in_dim(part, owner * block_size, block_size, 1)
                for part in (real_part, imag_part)
            ]
        )

    sums = m_block(lon_index)
    arrived = [
        rotated(m_block((lon_index + by) % lon_count).astype(jnp.bfloat16), "lon", by)
        for by in range(1, lon_count)
    ]
    for block in arrived:
        sums = sums + block.astype(jnp.float32)
    spectra = sums.astype(jnp.bfloat16).reshape(2, cycles_dev, channels, block_size)
    spectra = jnp.transpose(spectra, (1, 0, 2, 3)).reshape(cycles_dev, 2 * channels, 1, block_size)
    spec_rows = jnp.broadcast_to(
        spectra.astype(jnp.float32), (cycles_dev, 2 * channels, 8, block_size)
    )

    share = degrees // lat_count
    padded = padded_cycle(sky_map, width)
    weights = jnp.transpose(conv_weight, (1, 0, 2)).reshape(channels, -1)
    operands = legendre, spec_rows, weights, padded
    highest = degrees // block_size - 1
    choices = [(0, *middle, highest) for middle in FLOORS]
    if len(choices[0]) != lon_count:
        choices = [tuple(range(lon_count))]
    builds = [
        functools.partial(
            lat_sums,
            Plan(floors, lon_count, lat_count // 2, degrees, block_size),
            number,
            conv_shape=sky_map.shape,
        )
        for number, floors in enumerate(choices)
    ]
    if len(builds) == 1:
        summed, local_conv = builds[0](*operands)
    else:
        fits = jnp.all(jnp.array(choices, jnp.int32) <= block_ids[None, :], axis=1)
        best = jnp.max(jnp.where(fits, jnp.arange(len(choices), dtype=jnp.int32), 0))
        summed, local_conv = lax.switch(best, builds, *operands)
    degree_ids = lat_index * share + jnp.arange(share, dtype=jnp.int32)
    own_orders = lax.dynamic_slice_in_dim(orders, lon_index * block_size, block_size, 0)
    harmonics = jnp.where(
        degree_ids[:, None, None] >= own_orders[None, None, :], summed, jnp.float32(0.0)
    )
    return harmonics, local_conv


def solution(mesh):
    return jax.shard_map(
        on_device,
        mesh=mesh,
        in_specs=(P("lat", None, "lon"), P("lat", None, "lon"), P(), P()),
        out_specs=(P("lat", None, "lon"), P("lat", None, "lon")),
        check_vma=False,
    )
```
